32 devices in a mesh: mp: 4 (over x, core), seq: 8 (over z, y).
Axes of the slice: x: 2, y: 2, z: 4, core: 2. Of those that a mesh axis runs over, the one named last changes fastest.
Arguments:
- hidden_in: bfloat16 [2048, 5376], P('seq', 'mp'), may hold values from -28 to 28
- gain_in: float32 [5376], replicated, may hold values from 0.3 to 3
- w_query: bfloat16 [5376, 4096], P('seq', 'mp'), may hold values from -0.078125 to 0.078125
- key_weight: bfloat16 [5376, 2048], P('seq', 'mp'), may hold values from -0.078125 to 0.078125
- value_weight: bfloat16 [5376, 2048], P('seq', 'mp'), may hold values from -0.078125 to 0.078125
- gain_query: float32 [128], replicated, may hold values from 0.3 to 3
- gain_key: float32 [128], replicated, may hold values from 0.3 to 3
- start_pos: int32 [1], replicated, may hold values from 1024 to 4095
- cached_key_rows: bfloat16 [1024, 2048], P(None, 'mp'), may hold values from -140 to 140
- cached_value_rows: bfloat16 [1024, 2048], P(None, 'mp'), may hold values from -5 to 5
- w_out: bfloat16 [4096, 5376], P('seq', 'mp'), may hold values from -1.5 to 1.5
- gain_post: float32 [5376], P('mp'), may hold values from 0.3 to 3
Outputs:
- hidden_out: bfloat16 [2048, 5376], P('seq', 'mp')
The draws below stay inside these ranges and needn't reach their ends.
All inputs are finite; a program needn't handle non-finite values.
Results may differ from the reference program's by a relative error of at most 0.012.
The reference program's roundings to bfloat16 on the way count: a program that leaves them out, or rounds other values in their place, can miss the bound.
Values may be sent and summed in bfloat16 or wider, within the bound.
A program may use at most 128 MiB of HBM per device.

```python
import math
import jax
import jax.numpy as jnp
from jax import lax

MODEL_WIDTH = 5376
QUERY_HEAD_COUNT = 32
KEY_VALUE_HEADS = 16
HEAD_SIZE = 128
WINDOW_LENGTH = 1024
STRETCH_TOKENS = 2048


def draw_hidden_in(key, part):
    streams = jax.random.split(key, 3)
    low = math.log(0.3)
    high = math.log(3.0)
    row_scale = jnp.exp(jax.random.uniform(streams[0], (STRETCH_TOKENS, 1), jnp.float32, low, high))
    col_scale = jnp.exp(jax.random.uniform(streams[1], (1, MODEL_WIDTH), jnp.float32, low, high))
    base = jax.random.truncated_normal(streams[2], -3.0, 3.0, (STRETCH_TOKENS, MODEL_WIDTH), jnp.float32)
    return (base * row_scale * col_scale).astype(jnp.bfloat16)


def draw_w_out(key, part):
    streams = jax.random.split(key, 2)
    fan_rows = QUERY_HEAD_COUNT * HEAD_SIZE
    col_scale = jnp.exp(jax.random.uniform(streams[0], (1, MODEL_WIDTH), jnp.float32, 0.0, math.log(10.0)))
    col_scale = col_scale * 3.0 ** (jnp.arange(MODEL_WIDTH, dtype=jnp.float32)[None, :] / MODEL_WIDTH)
    base = jax.random.truncated_normal(streams[1], -3.0, 3.0, (fan_rows, MODEL_WIDTH), jnp.float32)
    return jnp.clip(base * fan_rows ** (-0.5) * col_scale, -1.5, 1.5).astype(jnp.bfloat16)


def draw_cached_key_rows(key, part):
    streams = jax.random.split(key, 1)
    column_range = KEY_VALUE_HEADS * HEAD_SIZE
    base = jax.random.truncated_normal(streams[0], -4.0, 4.0, (WINDOW_LENGTH, column_range), jnp.float32)
    return base.astype(jnp.bfloat16)


def block_scale(rng, shape, cuts, low, largest):
    level, own = 1.0, jax.random.fold_in(rng, 6)
    for position, shards_of in cuts:
        steps = jnp.exp(jax.random.uniform(jax.random.fold_in(own, position), (shards_of,), jnp.float32, low / len(cuts), largest / len(cuts)))
        level = level * jnp.repeat(steps, shape[position] // shards_of).reshape([-1 if axis == position else 1 for axis in range(len(shape))])
    return level


def bell_draw(stream_key, extent, width, most, cuts=(), kind=jnp.bfloat16):
    entries = jax.random.normal(stream_key, extent, jnp.float32) * width
    if len(cuts) > 0:
        entries = block_scale(stream_key, extent, cuts, -0.22, 0.18) * entries
    return jnp.clip(entries, min=-most, max=most).astype(kind)


def setup_inputs(seed: int = 0) -> dict:
    seeds = jax.random.split(jax.random.key(seed), 13)
    return {
        "hidden_in": draw_hidden_in(jax.random.fold_in(seeds[12], 71), 0),
        "gain_in": jnp.clip(jnp.exp(jax.random.uniform(seeds[1], (MODEL_WIDTH,), jnp.float32, math.log(0.3), math.log(3.0))), 0.3, 3.0),
        "w_query": bell_draw(seeds[2], (MODEL_WIDTH, QUERY_HEAD_COUNT * HEAD_SIZE), MODEL_WIDTH ** -0.5, 0.078125, ((0, 8), (1, 4))),
        "key_weight": bell_draw(seeds[3], (MODEL_WIDTH, KEY_VALUE_HEADS * HEAD_SIZE), MODEL_WIDTH ** -0.5, 0.078125, ((0, 8), (1, 4))),
        "value_weight": bell_draw(seeds[4], (MODEL_WIDTH, KEY_VALUE_HEADS * HEAD_SIZE), MODEL_WIDTH ** -0.5, 0.078125, ((0, 8), (1, 4))),
        "gain_query": jnp.clip(jnp.exp(jax.random.uniform(seeds[5], (HEAD_SIZE,), jnp.float32, math.log(0.3), math.log(3.0))), 0.3, 3.0),
        "gain_key": jnp.clip(jnp.exp(jax.random.uniform(seeds[6], (HEAD_SIZE,), jnp.float32, math.log(0.3), math.log(3.0))), 0.3, 3.0),
        "start_pos": jax.random.randint(seeds[7], (1,), WINDOW_LENGTH, 4 * WINDOW_LENGTH).astype(jnp.int32),
        "cached_key_rows": draw_cached_key_rows(jax.random.fold_in(seeds[12], 71), 0),
        "cached_value_rows": bell_draw(seeds[9], (WINDOW_LENGTH, KEY_VALUE_HEADS * HEAD_SIZE), 1.0, 5.0, ((1, 4),)),
        "w_out": draw_w_out(jax.random.fold_in(seeds[12], 71), 0),
        "gain_post": jnp.clip(jnp.exp(math.log(3.0) - 2.3025851 * jax.random.uniform(seeds[11], (MODEL_WIDTH,), jnp.float32) ** block_scale(seeds[11], (MODEL_WIDTH,), ((0, 4),), -0.2, 0.2)), 0.3, 3.0),
    }


epsilon = 1e-06
query_scale = 168.0 ** (-0.5)
rope_base = 10000.0

def norm_rows(values, gain):
    return values * lax.rsqrt(lax.optimization_barrier(jnp.mean(values * values, axis=-1, keepdims=True)) + epsilon) * gain

def rotate(tensor, positions):
    half_dim = tensor.shape[-1] // 2
    inverse_freq = rope_base ** (-(jnp.arange(half_dim, dtype=jnp.float32) * 2.0) / tensor.shape[-1])
    angles = positions.astype(jnp.float32)[:, None, None] * inverse_freq[None, None, :]
    cosine = jnp.cos(angles)
    sine = jnp.sin(angles)
    first = tensor[..., :half_dim]
    second = tensor[..., half_dim:]
    return jnp.concatenate([first * cosine - second * sine, second * cosine + first * sine], axis=-1)

def reference(hidden_in, gain_in, w_query, key_weight, value_weight, gain_query, gain_key, start_pos, cached_key_rows, cached_value_rows, w_out, gain_post):
    residual_in = hidden_in.astype(jnp.float32)
    normed_hidden = norm_rows(residual_in, gain_in).astype(jnp.bfloat16)
    query_matrix = jnp.dot(normed_hidden, w_query, preferred_element_type=jnp.float32).reshape(STRETCH_TOKENS, QUERY_HEAD_COUNT, HEAD_SIZE)
    stretch_keys = jnp.dot(normed_hidden, key_weight, preferred_element_type=jnp.float32).reshape(STRETCH_TOKENS, KEY_VALUE_HEADS, HEAD_SIZE)
    stretch_values = jnp.dot(normed_hidden, value_weight, preferred_element_type=jnp.float32).astype(jnp.bfloat16).reshape(STRETCH_TOKENS, KEY_VALUE_HEADS, HEAD_SIZE)
    positions = start_pos[0] + jnp.arange(STRETCH_TOKENS, dtype=jnp.int32)
    query_matrix = (rotate(norm_rows(query_matrix, gain_query), positions) * query_scale).astype(jnp.bfloat16)
    stretch_keys = rotate(norm_rows(stretch_keys, gain_key), positions).astype(jnp.bfloat16)
    joined_keys = jnp.concatenate([cached_key_rows.reshape(WINDOW_LENGTH, KEY_VALUE_HEADS, HEAD_SIZE), stretch_keys], axis=0)
    joined_values = jnp.concatenate([cached_value_rows.reshape(WINDOW_LENGTH, KEY_VALUE_HEADS, HEAD_SIZE), stretch_values], axis=0)
    query_group_count = QUERY_HEAD_COUNT // KEY_VALUE_HEADS
    block_list = STRETCH_TOKENS // WINDOW_LENGTH
    grouped_queries = query_matrix.reshape(block_list, WINDOW_LENGTH, KEY_VALUE_HEADS, query_group_count, HEAD_SIZE)

    def one_block(inputs):
        query_block, block_index = inputs
        key_block = lax.dynamic_slice_in_dim(joined_keys, block_index * WINDOW_LENGTH, 2 * WINDOW_LENGTH, 0)
        value_block = lax.dynamic_slice_in_dim(joined_values, block_index * WINDOW_LENGTH, 2 * WINDOW_LENGTH, 0)
        scores = jnp.einsum('tkgd,skd->kgts', query_block.astype(jnp.float32), key_block.astype(jnp.float32))
        query_index = jnp.arange(WINDOW_LENGTH, dtype=jnp.int32)[:, None]
        key_index = jnp.arange(2 * WINDOW_LENGTH, dtype=jnp.int32)[None, :]
        visible = (key_index > query_index) & (key_index <= query_index + WINDOW_LENGTH)
        scores = jnp.where(visible, scores, -jnp.inf)
        row_max = lax.optimization_barrier(jnp.max(scores, axis=-1, keepdims=True))
        probs = jnp.exp(scores - row_max)
        totals = lax.optimization_barrier(jnp.sum(probs, axis=-1))
        probs_b = probs.astype(jnp.bfloat16)
        summed = jnp.einsum('kgts,skd->tkgd', probs_b.astype(jnp.float32), value_block.astype(jnp.float32))
        summed = summed / jnp.transpose(totals, (2, 0, 1))[..., None]
        return summed.reshape(WINDOW_LENGTH, QUERY_HEAD_COUNT * HEAD_SIZE).astype(jnp.bfloat16)
    attn = lax.map(one_block, (grouped_queries, jnp.arange(block_list, dtype=jnp.int32))).reshape(STRETCH_TOKENS, QUERY_HEAD_COUNT * HEAD_SIZE)
    mixed = jnp.dot(attn, w_out, preferred_element_type=jnp.float32)
    return (residual_in + norm_rows(mixed, gain_post)).astype(jnp.bfloat16)
```

```python
import functools

import jax
import jax.numpy as jnp
from jax import lax
from jax.experimental import pallas as pl
from jax.experimental.pallas import tpu as pltpu
from jax.sharding import PartitionSpec as P

MODEL_WIDTH = 5376
WINDOW_LENGTH = 1024


epsilon = 1e-06
query_scale = 168.0 ** (-0.5)
rope_base = 10000.0

MESH = pl.DeviceIdType.MESH
f32 = jnp.float32
bf16 = jnp.bfloat16


def layer_kernel(
    hidden, gain_in, wq, wk, wv, gain_q, gain_k, cos_t, sin_t, cache_k, cache_v, wo, gain_post,
    out,
    xb, wb, ob, kv, qb, ab, rb, sb, ss,
    local_sem, xz_send, xz_recv, xx_send, xx_recv, xc_send, xc_recv,
    wz_send, wz_recv, wy_send, wy_recv, oz_send, oz_recv, oy_send, oy_recv,
    kv_send, kv_recv, a_send, a_recv, r_send, r_recv, s_send, s_recv,
):
    NZ, NM = 4, 4
    rows, cols = hidden.shape
    depth = wq.shape[0]
    m = lax.axis_index("mp")
    s = lax.axis_index("seq")
    z, y = s // 2, s % 2
    x, c = m // 2, m % 2
    ypeer = {"mp": m, "seq": 2 * z + (1 - y)}
    xpeer_m = (1 - x) * 2 + c
    cpeer_m = x * 2 + (1 - c)
    xpeer = {"mp": xpeer_m, "seq": s}
    cpeer = {"mp": cpeer_m, "seq": s}
    head = (z + 4 - m) % 4

    def at_z(zz):
        return {"mp": m, "seq": 2 * zz + y}

    def remote(src, dst, send, recv, dev):
        return pltpu.make_async_remote_copy(
            src_ref=src, dst_ref=dst, send_sem=send, recv_sem=recv,
            device_id=dev, device_id_type=MESH)

    barrier = pltpu.get_barrier_semaphore()
    for d in range(1, 4):
        pl.semaphore_signal(barrier, inc=1, device_id=at_z((z + d) % 4), device_id_type=MESH)
        pl.semaphore_signal(barrier, inc=1, device_id={"mp": (m + d) % 4, "seq": s}, device_id_type=MESH)
    pl.semaphore_signal(barrier, inc=1, device_id=ypeer, device_id_type=MESH)

    k_own = head
    locals_ = [
        (None, pltpu.make_async_copy(hidden, xb.at[z, m], local_sem.at[0])),
        (None, pltpu.make_async_copy(cache_k.at[:, pl.ds(pl.multiple_of(head * 128, 128), 128)], kv.at[pl.ds(0, 1024), pl.ds(0, 128)], local_sem.at[1])),
        (None, pltpu.make_async_copy(cache_v.at[:, pl.ds(pl.multiple_of(head * 128, 128), 128)], kv.at[pl.ds(0, 1024), pl.ds(128, 128)], local_sem.at[2])),
    ]

    def w_parts(k, zsrc):
        r0 = pl.ds(pl.multiple_of(y * depth, 16), depth)
        return [
            (wq.at[:, pl.ds(pl.multiple_of(k * 256, 128), 256)], wb.at[zsrc, r0, pl.ds(0, 256)]),
            (wk.at[:, pl.ds(pl.multiple_of(k * 128, 128), 128)], wb.at[zsrc, r0, pl.ds(256, 128)]),
            (wv.at[:, pl.ds(pl.multiple_of(k * 128, 128), 128)], wb.at[zsrc, r0, pl.ds(384, 128)]),
        ]

    for i, (a, b) in enumerate(w_parts(k_own, z)):
        locals_.append((None, pltpu.make_async_copy(a, b, local_sem.at[3 + i])))
    o_half = []
    for h in range(2):
        zd = (2 * y + h + z) % 4
        o_half.append((zd, wo.at[pl.ds(h * 256, 256), :], ob.at[z]))
        cp = pltpu.make_async_copy(wo.at[pl.ds(h * 256, 256), :], ob.at[z], local_sem.at[6])
        locals_.append((zd == z, cp))

    def when(cond, fn):
        if cond is None:
            fn()
        else:
            pl.when(cond)(fn)

    for cond, cp in locals_:
        when(cond, cp.start)

    pl.semaphore_wait(barrier, 7)

    pending = []

    def send(cond, cp):
        when(cond, cp.start)
        pending.append((cond, cp))

    def x_right(zz):
        return remote(xb.at[zz, m], xb.at[zz, m], xz_send.at[0, zz], xz_recv.at[zz], at_z((z + 1) % 4))

    def x_left(zz):
        return remote(xb.at[zz, m], xb.at[zz, m], xz_send.at[1, zz], xz_recv.at[zz], at_z((z + 3) % 4))

    def x_x(zz):
        return remote(xb.at[zz, m], xb.at[zz, m], xx_send.at[zz], xx_recv.at[zz], xpeer)

    def x_c(zz, mm, which):
        return remote(xb.at[zz, mm], xb.at[zz, mm], xc_send.at[which, zz], xc_recv.at[which, zz], cpeer)

    locals_[0][1].wait()
    send(z < 3, x_right(z))
    send(z > 0, x_left(z))
    for d in (2, 1, 3):
        zd = (z + d) % 4
        k = (zd + 4 - m) % 4
        for i, (a, b) in enumerate(w_parts(k, z)):
            send(None, remote(a, b, wz_send.at[d, i], wz_recv.at[z, i], at_z(zd)))
    send(None, x_x(z))
    send(None, x_c(z, m, 0))
    for h in range(2):
        zd, a, b = o_half[h]
        send(zd != z, remote(a, b, oz_send.at[h], oz_recv.at[z], at_z(zd)))

    def w_forward(zsrc, sem):
        r0 = pl.ds(pl.multiple_of(y * depth, 16), depth)
        return remote(wb.at[zsrc, r0, :], wb.at[zsrc, r0, :], wy_send.at[sem], wy_recv.at[zsrc], ypeer)

    for i in range(3):
        locals_[3 + i][1].wait()
    send(None, w_forward(z, 0))

    def x_from(cond, zz):
        def arrived():
            x_right(zz).wait_recv()
        when(cond, arrived)

    def x_from_x(cond, zz):
        def arrived():
            x_x(zz).wait_recv()
        when(cond, arrived)
        send(cond, x_c(zz, xpeer_m, 1))

    x_from_x(None, z)
    for d in range(1, 4):
        left, right = z - d, z + d
        lz, rz = (z + 4 - d) % 4, (z + d) % 4
        x_from(left >= 0, lz)
        send((left >= 0) & (z < 3), x_right(lz))
        send(left >= 0, x_x(lz))
        send(left >= 0, x_c(lz, m, 0))
        x_from(right <= 3, rz)
        send((right <= 3) & (z > 0), x_left(rz))
        send(right <= 3, x_x(rz))
        send(right <= 3, x_c(rz, m, 0))
        zs = (z + 4 - d) % 4
        for i, (a, b) in enumerate(w_parts(0, zs)):
            remote(b, b, wz_send.at[0, i], wz_recv.at[zs, i], ypeer).wait_recv()
        send(None, w_forward(zs, d))
        x_from_x(left >= 0, lz)
        x_from_x(right <= 3, rz)

    for zs in range(4):
        mine = ((z + 4 - zs) % 4) // 2 == y
        own = zs == z
        ow = remote(ob.at[zs], ob.at[zs], oz_send.at[0], oz_recv.at[zs], ypeer)
        when(mine & (zs != z), ow.wait_recv)
        when(mine & own, pltpu.make_async_copy(ob.at[zs], ob.at[zs], local_sem.at[6]).wait)
        send(mine, remote(ob.at[zs], ob.at[zs], oy_send.at[zs], oy_recv.at[zs], ypeer))

    for zs in range(4):
        for which in range(2):
            mm = cpeer_m if which == 0 else (1 - x) * 2 + (1 - c)
            remote(xb.at[zs, mm], xb.at[zs, mm], xc_send.at[which, zs], xc_recv.at[which, zs], cpeer).wait_recv()
        r1 = pl.ds(pl.multiple_of((1 - y) * depth, 16), depth)
        remote(wb.at[zs, r1, :], wb.at[zs, r1, :], wy_send.at[zs], wy_recv.at[zs], ypeer).wait_recv()

    def kv_copy(b):
        r = pl.ds(pl.multiple_of(1024 + (2 * b + y) * 256, 256), 256)
        return remote(kv.at[r, :], kv.at[r, :], kv_send.at[b], kv_recv.at[b], ypeer)

    def head_norm(g, gain, cosine, sine):
        g = g * lax.rsqrt(jnp.mean(g * g, axis=-1, keepdims=True) + epsilon) * gain
        return g * cosine + pltpu.roll(g, 64, 1) * sine

    def project(b, carry):
        total = jnp.zeros((rows, 1), f32)
        for mm in range(NM):
            v = xb[b, mm].astype(f32)
            total += jnp.sum(v * v, axis=-1, keepdims=True)
        scale = lax.rsqrt(total / MODEL_WIDTH + epsilon)
        acc = jnp.zeros((rows, 512), f32)
        for mm in range(NM):
            n = (xb[b, mm].astype(f32) * scale * gain_in[mm]).astype(bf16)
            acc += jnp.dot(n, wb[mm], preferred_element_type=f32)
        r = pl.ds(pl.multiple_of(b * rows, rows), rows)
        cosine, sine = cos_t[r, :], sin_t[r, :]
        for h in range(2):
            q = head_norm(acc[:, h * 128:(h + 1) * 128], gain_q[...], cosine, sine) * query_scale
            qb[h, r, :] = q.astype(bf16)
        rk = pl.ds(pl.multiple_of(1024 + (2 * b + y) * 256, 256), 256)
        kv[rk, 0:128] = head_norm(acc[:, 256:384], gain_k[...], cosine, sine).astype(bf16)
        kv[rk, 128:256] = acc[:, 384:512].astype(bf16)
        kv_copy(b).start()
        return carry

    lax.fori_loop(0, NZ, project, 0)
    locals_[1][1].wait()
    locals_[2][1].wait()

    def kv_wait(b, carry):
        r = pl.ds(pl.multiple_of(1024 + (2 * b + (1 - y)) * 256, 256), 256)
        remote(kv.at[r, :], kv.at[r, :], kv_send.at[b], kv_recv.at[b], ypeer).wait_recv()
        kv_copy(b).wait_send()
        return carry

    lax.fori_loop(0, NZ, kv_wait, 0)

    def a_copy(b, d):
        r = pl.ds(pl.multiple_of(b * rows, rows), rows)
        return remote(ab.at[m, r, :], ab.at[m, r, :], a_send.at[b, d], a_recv.at[b, m],
                      {"mp": (m + d) % 4, "seq": s})

    def attend(b, carry):
        r = pl.ds(pl.multiple_of(b * rows, rows), rows)
        span = WINDOW_LENGTH + 256
        rk = pl.ds(pl.multiple_of((2 * b + y) * 256, 256), span)
        keys = kv[rk, 0:128]
        vals = kv[rk, 128:256]
        qi = lax.broadcasted_iota(jnp.int32, (rows, span), 0)
        ei = lax.broadcasted_iota(jnp.int32, (rows, span), 1)
        visible = (ei > qi) & (ei <= qi + WINDOW_LENGTH)
        for h in range(2):
            sc = lax.dot_general(qb[h, r, :], keys, (((1,), (1,)), ((), ())), preferred_element_type=f32)
            sc = jnp.where(visible, sc, -jnp.inf)
            top = jnp.max(sc, axis=-1, keepdims=True)
            p = jnp.exp(sc - top)
            tot = jnp.sum(p, axis=-1, keepdims=True)
            o = jnp.dot(p.astype(bf16), vals, preferred_element_type=f32)
            ab[m, r, h * 128:(h + 1) * 128] = (o / tot).astype(bf16)
        for d in range(1, 4):
            a_copy(b, d).start()
        return carry

    lax.fori_loop(0, NZ, attend, 0)

    for zs in range(4):
        other = ((z + 4 - zs) % 4) // 2 != y
        when(other, remote(ob.at[zs], ob.at[zs], oy_send.at[zs], oy_recv.at[zs], ypeer).wait_recv)

    def a_wait(b, carry):
        r = pl.ds(pl.multiple_of(b * rows, rows), rows)
        for d in range(1, 4):
            mm = (m + d) % 4
            remote(ab.at[mm, r, :], ab.at[mm, r, :], a_send.at[b, d], a_recv.at[b, mm], ypeer).wait_recv()
            a_copy(b, d).wait_send()
        return carry

    lax.fori_loop(0, NZ, a_wait, 0)

    def partial(b):
        r = pl.ds(pl.multiple_of(b * rows, rows), rows)
        acc = jnp.dot(ab[0, r, :], ob[0], preferred_element_type=f32)
        for mm in range(1, NM):
            acc += jnp.dot(ab[mm, r, :], ob[mm], preferred_element_type=f32)
        return acc

    def r_copy(side, d, zd):
        return remote(sb.at[d], rb.at[side, d], r_send.at[d], r_recv.at[side, d], at_z(zd))

    def hop(side, d, inner):
        def go():
            sb[d] = partial(d).astype(bf16)

            def add():
                r_copy(side, d, z).wait_recv()
                sb[d] = (partial(d) + rb[side, d].astype(f32)).astype(bf16)
            pl.when(inner)(add)
            r_copy(side, d, (z + 1) % 4 if side == 0 else (z + 3) % 4).start()
        return go

    for i in range(3):
        dr, dl = 3 - i, i
        pl.when(z < dr)(hop(0, dr, z > 0))
        pl.when(z > dl)(hop(1, dl, z < 3))

    out_acc = xb.shape and partial(z)
    ss_acc = out_acc
    zero = jnp.zeros_like(out_acc)

    @pl.when(z > 0)
    def _():
        r_copy(0, z, (z + 1) % 4).wait_recv()

    @pl.when(z == 0)
    def _():
        rb[0, z] = zero.astype(bf16)

    @pl.when(z < 3)
    def _():
        r_copy(1, z, (z + 1) % 4).wait_recv()

    @pl.when(z == 3)
    def _():
        rb[1, z] = zero.astype(bf16)

    mixed = ss_acc + rb[0, z].astype(f32) + rb[1, z].astype(f32)
    ss[m] = jnp.broadcast_to(jnp.sum(mixed * mixed, axis=-1, keepdims=True), (rows, 128))

    def s_copy(d):
        return remote(ss.at[m], ss.at[m], s_send.at[d], s_recv.at[m], {"mp": (m + d) % 4, "seq": s})

    for d in range(1, 4):
        s_copy(d).start()
    for d in range(1, 4):
        mm = (m + d) % 4
        remote(ss.at[mm], ss.at[mm], s_send.at[d], s_recv.at[mm], ypeer).wait_recv()
    squares = (ss[0] + ss[1] + ss[2] + ss[3])[:, 0:1]
    scaling = lax.rsqrt(squares / MODEL_WIDTH + epsilon)
    out[...] = (xb[z, m].astype(f32) + mixed * scaling * gain_post[...]).astype(bf16)

    for d in range(1, 4):
        s_copy(d).wait_send()
    for d in range(4):
        when(z != d, r_copy(0, d, (z + 1) % 4).wait_send)
    for cond, cp in pending:
        when(cond, cp.wait_send)


def fused(
    hidden_in, gain_in, w_query, key_weight, value_weight, gain_query, gain_key, start_pos,
    cached_key_rows, cached_value_rows, w_out, gain_post,
):
    rows, cols = hidden_in.shape
    depth = w_query.shape[0]
    y = lax.axis_index("seq") % 2
    block = jnp.arange(4, dtype=jnp.int32)[:, None] * 2 + y
    positions = (start_pos[0] + block * rows + jnp.arange(rows, dtype=jnp.int32)[None, :]).reshape(-1)
    inverse_freq = rope_base ** (-(jnp.arange(64, dtype=f32) * 2.0) / 128)
    angles = positions.astype(f32)[:, None] * inverse_freq[None, :]
    cosine, sine = jnp.cos(angles), jnp.sin(angles)
    cos_t = jnp.concatenate([cosine, cosine], axis=1)
    sin_t = jnp.concatenate([-sine, sine], axis=1)
    hbm = pl.BlockSpec(memory_space=pl.ANY)
    vmem = pl.BlockSpec(memory_space=pltpu.VMEM)
    dma = pltpu.SemaphoreType.DMA
    return pl.pallas_call(
        layer_kernel,
        name="layer",
        out_shape=jax.ShapeDtypeStruct((rows, cols), bf16),
        in_specs=[hbm, vmem, hbm, hbm, hbm, vmem, vmem, vmem, vmem, hbm, hbm, hbm, vmem],
        out_specs=vmem,
        scratch_shapes=[
            pltpu.VMEM((4, 4, rows, cols), bf16),
            pltpu.VMEM((4, 2 * depth, 512), bf16),
            pltpu.VMEM((4, 256, cols), bf16),
            pltpu.VMEM((3072, 256), bf16),
            pltpu.VMEM((2, 1024, 128), bf16),
            pltpu.VMEM((4, 1024, 256), bf16),
            pltpu.VMEM((2, 4, rows, cols), bf16),
            pltpu.VMEM((4, rows, cols), bf16),
            pltpu.VMEM((4, rows, 128), f32),
            dma((7,)), dma((2, 4)), dma((4,)), dma((4,)), dma((4,)), dma((2, 4)), dma((2, 4)),
            dma((4, 3)), dma((4, 3)), dma((4,)), dma((4,)), dma((2,)), dma((4,)), dma((4,)), dma((4,)),
            dma((4,)), dma((4,)), dma((4, 4)), dma((4, 4)), dma((4,)), dma((2, 4)), dma((4,)), dma((4,)),
        ],
        compiler_params=pltpu.CompilerParams(
            collective_id=0, has_side_effects=True, vmem_limit_bytes=56 * 1024 * 1024,
        ),
    )(
        hidden_in, gain_in.reshape(4, 1, cols), w_query, key_weight, value_weight,
        gain_query.reshape(1, 128), gain_key.reshape(1, 128), cos_t, sin_t,
        cached_key_rows, cached_value_rows, w_out, gain_post.reshape(1, cols),
    )


def shifted(x, axis, by):
    peers = lax.axis_size(axis)
    pairs = [(i, i + by) for i in range(peers) if 0 <= i + by < peers]
    return lax.ppermute(x, axis, pairs)


def norm_rows(values, gain):
    return values * lax.rsqrt(jnp.mean(values * values, axis=-1, keepdims=True) + epsilon) * gain


def rotate(tensor, positions):
    half_dim = tensor.shape[-1] // 2
    inverse_freq = rope_base ** (
        -(jnp.arange(half_dim, dtype=jnp.float32) * 2.0) / tensor.shape[-1]
    )
    angles = positions.astype(jnp.float32)[:, None, None] * inverse_freq[None, None, :]
    cosine = jnp.cos(angles)
    sine = jnp.sin(angles)
    first = tensor[..., :half_dim]
    second = tensor[..., half_dim:]
    return jnp.concatenate(
        [first * cosine - second * sine, second * cosine + first * sine], axis=-1
    )


def on_device(
    hidden_in,
    gain_in,
    w_query,
    key_weight,
    value_weight,
    gain_query,
    gain_key,
    start_pos,
    cached_key_rows,
    cached_value_rows,
    w_out,
    gain_post,
):
    n_rows = hidden_in.shape[0]
    head_dim = gain_query.shape[0]
    kv_cols = key_weight.shape[1]
    kv_heads = kv_cols // head_dim
    q_heads = w_query.shape[1] // head_dim
    query_group_count = q_heads // kv_heads
    full_rows = lax.all_gather(hidden_in, "mp", axis=1, tiled=True)
    normed_hidden = norm_rows(full_rows.astype(jnp.float32), gain_in).astype(jnp.bfloat16)

    def add_rows(block_rows):
        return jnp.dot(normed_hidden, block_rows, preferred_element_type=jnp.float32)

    keys_raw = add_rows(lax.all_gather(key_weight, "seq", axis=0, tiled=True))
    values_raw = add_rows(lax.all_gather(value_weight, "seq", axis=0, tiled=True))
    query_matrix = add_rows(lax.all_gather(w_query, "seq", axis=0, tiled=True))
    seq_index = lax.axis_index("seq")
    positions = start_pos[0] + seq_index * n_rows + jnp.arange(n_rows, dtype=jnp.int32)
    query_matrix = (
        rotate(norm_rows(query_matrix.reshape(n_rows, q_heads, head_dim), gain_query), positions)
        * query_scale
    ).astype(jnp.bfloat16)
    fresh_key = rotate(
        norm_rows(keys_raw.reshape(n_rows, kv_heads, head_dim), gain_key), positions
    ).astype(jnp.bfloat16)
    fresh = jnp.stack([fresh_key.reshape(n_rows, kv_cols), values_raw.astype(jnp.bfloat16)])
    reach_shards = (WINDOW_LENGTH + n_rows - 1) // n_rows
    reach_rows = reach_shards * n_rows
    pieces = []
    moving = fresh
    for hop_index in range(reach_shards):
        moving = shifted(moving, "seq", 1)
        pieces.insert(0, moving)
    prior = jnp.concatenate(pieces, axis=1)
    front_pad = reach_rows - WINDOW_LENGTH
    cached = jnp.stack([cached_key_rows, cached_value_rows])
    padded = jnp.concatenate(
        [
            jnp.zeros((2, front_pad, kv_cols), cached.dtype),
            cached,
            jnp.zeros((2, reach_rows, kv_cols), cached.dtype),
        ],
        axis=1,
    )
    cache_start = jnp.minimum(seq_index * n_rows, front_pad + WINDOW_LENGTH)
    from_cache = lax.dynamic_slice_in_dim(padded, cache_start, reach_rows, 1)
    prior_rows = jnp.arange(reach_rows, dtype=jnp.int32)
    use_cache = prior_rows < reach_rows - seq_index * n_rows
    prior = jnp.where(use_cache[None, :, None], from_cache, prior)
    window_kv = jnp.concatenate([prior, fresh], axis=1)
    span_rows = reach_rows + n_rows
    key_heads = window_kv[0].reshape(span_rows, kv_heads, head_dim)
    value_heads = window_kv[1].reshape(span_rows, kv_heads, head_dim)
    query_heads = query_matrix.reshape(n_rows, kv_heads, query_group_count, head_dim)
    scores = jnp.einsum(
        "tkgd,skd->kgts", query_heads, key_heads, preferred_element_type=jnp.float32
    )
    query_index = jnp.arange(n_rows, dtype=jnp.int32)[:, None]
    key_index = jnp.arange(span_rows, dtype=jnp.int32)[None, :]
    visible = (key_index > query_index + reach_rows - WINDOW_LENGTH) & (
        key_index <= query_index + reach_rows
    )
    scores = jnp.where(visible, scores, -jnp.inf)
    row_max = jnp.max(scores, axis=-1, keepdims=True)
    probs = jnp.exp(scores - row_max)
    totals = jnp.sum(probs, axis=-1)
    probs_b = probs.astype(jnp.bfloat16)
    summed = jnp.einsum("kgts,skd->tkgd", probs_b, value_heads, preferred_element_type=jnp.float32)
    summed = summed / jnp.transpose(totals, (2, 0, 1))[..., None]
    attn = summed.reshape(n_rows, q_heads * head_dim).astype(jnp.bfloat16)
    all_heads = lax.all_gather(attn, "mp", axis=1, tiled=True)
    projected = jnp.dot(
        all_heads,
        lax.all_gather(w_out, "seq", axis=0, tiled=True),
        preferred_element_type=jnp.float32,
    )
    squares = lax.psum(jnp.sum(projected * projected, axis=-1), "mp")
    scaling = lax.rsqrt(squares / MODEL_WIDTH + epsilon)
    return (hidden_in.astype(jnp.float32) + projected * scaling[:, None] * gain_post).astype(
        jnp.bfloat16
    )


def solution(mesh):
    in_specs = (
        P("seq", "mp"),
        P(),
        P("seq", "mp"),
        P("seq", "mp"),
        P("seq", "mp"),
        P(),
        P(),
        P(),
        P(None, "mp"),
        P(None, "mp"),
        P("seq", "mp"),
        P("mp"),
    )
    out_specs = P("seq", "mp")
    fits = mesh.shape["mp"] == 4 and mesh.shape["seq"] == 8
    return jax.shard_map(
        fused if fits else on_device, mesh=mesh, in_specs=in_specs, out_specs=out_specs, check_vma=False
    )
```

```python
import functools

import jax
import jax.numpy as jnp
from jax import lax
from jax.experimental import pallas as pl
from jax.experimental.pallas import tpu as pltpu
from jax.sharding import PartitionSpec as P

MODEL_WIDTH = 5376
WINDOW_LENGTH = 1024


epsilon = 1e-06
query_scale = 168.0 ** (-0.5)
rope_base = 10000.0

MESH = pl.DeviceIdType.MESH
f32 = jnp.float32
bf16 = jnp.bfloat16


def layer_kernel(
    hidden, gain_in, wq, wk, wv, gain_q, gain_k, cos_t, sin_t, cache_k, cache_v, wo, gain_post,
    out,
    xb, xn, tb, wb, ob, kv, qb, ab, rb, sb, ss, pacc,
    local_sem, xz_send, xz_recv, xx_send, xx_recv, xc_send, xc_recv,
    t_send, t_recv, wz_send, wz_recv, wy_send, wy_recv, c_send, c_recv, oy_send, oy_recv,
    kv_send, kv_recv, a_send, a_recv, r_send, r_recv, s_send, s_recv,
):
    NZ, NM = 4, 4
    rows, cols = hidden.shape
    depth = wq.shape[0]
    m = lax.axis_index("mp")
    s = lax.axis_index("seq")
    z, y = s // 2, s % 2
    x, c = m // 2, m % 2
    ypeer = {"mp": m, "seq": 2 * z + (1 - y)}
    xpeer_m = (1 - x) * 2 + c
    cpeer_m = x * 2 + (1 - c)
    xpeer = {"mp": xpeer_m, "seq": s}
    cpeer = {"mp": cpeer_m, "seq": s}

    def at_z(zz):
        return {"mp": m, "seq": 2 * zz + y}

    def remote(src, dst, send, recv, dev):
        return pltpu.make_async_remote_copy(
            src_ref=src, dst_ref=dst, send_sem=send, recv_sem=recv,
            device_id=dev, device_id_type=MESH)

    barrier = pltpu.get_barrier_semaphore()
    for d in range(1, 4):
        pl.semaphore_signal(barrier, inc=1, device_id=at_z((z + d) % 4), device_id_type=MESH)
        pl.semaphore_signal(barrier, inc=1, device_id={"mp": (m + d) % 4, "seq": s}, device_id_type=MESH)
    pl.semaphore_signal(barrier, inc=1, device_id=ypeer, device_id_type=MESH)

    def w_parts(j, k):
        return [
            (wq.at[:, pl.ds(pl.multiple_of(j * 256, 128), 256)], tb.at[k, :, pl.ds(0, 256)]),
            (wk.at[:, pl.ds(pl.multiple_of(j * 128, 128), 128)], tb.at[k, :, pl.ds(256, 128)]),
            (wv.at[:, pl.ds(pl.multiple_of(j * 128, 128), 128)], tb.at[k, :, pl.ds(384, 128)]),
        ]

    def wb_at(zsrc, yy):
        return wb.at[zsrc, pl.ds(pl.multiple_of(yy * depth, 16), depth), :]

    def c_parts(j):
        return [
            (cache_k.at[:, pl.ds(j * 128, 128)], kv.at[pl.ds(0, 1024), pl.ds(0, 128)]),
            (cache_v.at[:, pl.ds(j * 128, 128)], kv.at[pl.ds(0, 1024), pl.ds(128, 128)]),
        ]

    locals_ = [(None, pltpu.make_async_copy(hidden, xb.at[z, m], local_sem.at[0]))]
    own_w = [
        (None, pltpu.make_async_copy(a, b, local_sem.at[1 + i])) for i, (a, b) in enumerate(w_parts(m, m))
    ]
    own_c = []
    for j in range(4):
        mine = (m == j) & (z == j)
        own_c.extend((mine, pltpu.make_async_copy(a, b, local_sem.at[4 + i])) for i, (a, b) in enumerate(c_parts(j)))
    own_o = [
        (None, pltpu.make_async_copy(wo.at[pl.ds(h * 256, 256), :], ob.at[2 * y + h], local_sem.at[6 + h]))
        for h in range(2)
    ]
    locals_ = locals_ + own_w + own_c + own_o

    def when(cond, fn):
        if cond is None:
            fn()
        else:
            pl.when(cond)(fn)

    for cond, cp in locals_:
        when(cond, cp.start)

    pl.semaphore_wait(barrier, 7)

    pending = []

    def send(cond, cp):
        when(cond, cp.start)
        pending.append((cond, cp))

    def x_right(zz):
        return remote(xb.at[zz, m], xb.at[zz, m], xz_send.at[0, zz], xz_recv.at[zz], at_z((z + 1) % 4))

    def x_left(zz):
        return remote(xb.at[zz, m], xb.at[zz, m], xz_send.at[1, zz], xz_recv.at[zz], at_z((z + 3) % 4))

    def x_x(zz):
        return remote(xb.at[zz, m], xb.at[zz, m], xx_send.at[zz], xx_recv.at[zz], xpeer)

    def x_c(zz, mm, which):
        return remote(xb.at[zz, mm], xb.at[zz, mm], xc_send.at[which, zz], xc_recv.at[which, zz], cpeer)

    def w_first(d):
        j = (m + d) % 4
        for i, (a, b) in enumerate(w_parts(j, m)):
            send(None, remote(a, b, t_send.at[d, i], t_recv.at[m, i], {"mp": j, "seq": s}))

    def w_second(k, d):
        for i, (a, b) in enumerate(w_parts(m, k)):
            remote(b, b, t_send.at[0, i], t_recv.at[k, i], ypeer).wait_recv()
        w_along(k, d)

    def w_along(k, d):
        send(k != z, remote(tb.at[k], wb_at(z, y), wz_send.at[d], wz_recv.at[z], at_z(k)))
        pl.when(k == z)(pltpu.make_async_copy(tb.at[k], wb_at(z, y), local_sem.at[8]).start)

    def w_third(zs, d):
        if d == 0:
            pltpu.make_async_copy(tb.at[z], wb_at(z, y), local_sem.at[8]).wait()
        else:
            remote(tb.at[z], wb_at(zs, y), wz_send.at[0], wz_recv.at[zs], ypeer).wait_recv()
        send(None, remote(wb_at(zs, y), wb_at(zs, y), wy_send.at[d], wy_recv.at[zs], ypeer))

    locals_[0][1].wait()
    send(z < 3, x_right(z))
    send(z > 0, x_left(z))
    w_first(2)
    w_first(1)
    w_first(3)
    for h in range(2):
        send(None, remote(wo.at[pl.ds(h * 256, 256), :], ob.at[2 * y + h], oy_send.at[h], oy_recv.at[h], ypeer))
    for _, cp in own_w:
        cp.wait()
    w_along(m, 0)
    send(None, x_c(z, m, 0))
    send(None, x_x(z))
    w_second(cpeer_m, 1)

    def x_step(d):
        left, right = z - d, z + d
        lz, rz = (z + 4 - d) % 4, (z + d) % 4
        when(left >= 0, x_right(lz).wait_recv)
        send((left >= 0) & (z < 3), x_right(lz))
        send(left >= 0, x_x(lz))
        send(left >= 0, x_c(lz, m, 0))
        when(right <= 3, x_right(rz).wait_recv)
        send((right <= 3) & (z > 0), x_left(rz))
        send(right <= 3, x_x(rz))
        send(right <= 3, x_c(rz, m, 0))

    def x_cross(d):
        left, right = z - d, z + d
        if d == 0:
            pairs = [(None, z)]
        else:
            pairs = [(left >= 0, (z + 4 - d) % 4), (right <= 3, (z + d) % 4)]
        for cond, zz in pairs:
            when(cond, x_x(zz).wait_recv)
            send(cond, x_c(zz, xpeer_m, 1))

    x_step(1)
    w_second(xpeer_m, 2)
    w_second((1 - x) * 2 + (1 - c), 3)
    w_third(z, 0)
    x_step(2)
    x_cross(0)
    w_third((z + 3) % 4, 1)
    w_third((z + 1) % 4, 2)
    x_step(3)
    x_cross(1)
    w_third((z + 2) % 4, 3)
    x_cross(2)
    x_cross(3)

    for j in range(4):
        for i, (a, b) in enumerate(c_parts(j)):
            send((m == z) & (m != j), remote(a, b, c_send.at[j, i], c_recv.at[i], {"mp": j, "seq": s}))
    for zs in range(4):
        for which in range(2):
            mm = cpeer_m if which == 0 else (1 - x) * 2 + (1 - c)
            remote(xb.at[zs, mm], xb.at[zs, mm], xc_send.at[which, zs], xc_recv.at[which, zs], cpeer).wait_recv()

    def norm_block(b, carry):
        total = jnp.zeros((rows, 1), f32)
        for mm in range(NM):
            v = xb[b, mm].astype(f32)
            total += jnp.sum(v * v, axis=-1, keepdims=True)
        scale = lax.rsqrt(total / MODEL_WIDTH + epsilon)
        for mm in range(NM):
            xn[b, mm] = (xb[b, mm].astype(f32) * scale * gain_in[mm]).astype(bf16)
        return carry

    lax.fori_loop(0, NZ, norm_block, 0)
    for zs in range(4):
        remote(wb_at(zs, 1 - y), wb_at(zs, 1 - y), wy_send.at[zs], wy_recv.at[zs], ypeer).wait_recv()

    def kv_copy(b):
        r = pl.ds(pl.multiple_of(1024 + (2 * b + y) * 256, 256), 256)
        return remote(kv.at[r, :], kv.at[r, :], kv_send.at[b], kv_recv.at[b], ypeer)

    def head_norm(g, gain, cosine, sine):
        g = g * lax.rsqrt(jnp.mean(g * g, axis=-1, keepdims=True) + epsilon) * gain
        return g * cosine + pltpu.roll(g, 64, 1) * sine

    def project(b, carry):
        acc = jnp.dot(xn[b, 0], wb[0], preferred_element_type=f32)
        for mm in range(1, NM):
            acc += jnp.dot(xn[b, mm], wb[mm], preferred_element_type=f32)
        r = pl.ds(pl.multiple_of(b * rows, rows), rows)
        cosine, sine = cos_t[r, :], sin_t[r, :]
        for h in range(2):
            q = head_norm(acc[:, h * 128:(h + 1) * 128], gain_q[...], cosine, sine) * query_scale
            qb[h, r, :] = q.astype(bf16)
        rk = pl.ds(pl.multiple_of(1024 + (2 * b + y) * 256, 256), 256)
        kv[rk, 0:128] = head_norm(acc[:, 256:384], gain_k[...], cosine, sine).astype(bf16)
        kv[rk, 128:256] = acc[:, 384:512].astype(bf16)
        kv_copy(b).start()
        return carry

    lax.fori_loop(0, NZ, project, 0)
    for i, (a, b) in enumerate(c_parts(0)):
        pl.when(m == z)(pltpu.make_async_copy(a, b, local_sem.at[4 + i]).wait)
        pl.when(m != z)(remote(b, b, c_send.at[0, i], c_recv.at[i], ypeer).wait_recv)

    def kv_wait(b, carry):
        r = pl.ds(pl.multiple_of(1024 + (2 * b + (1 - y)) * 256, 256), 256)
        remote(kv.at[r, :], kv.at[r, :], kv_send.at[b], kv_recv.at[b], ypeer).wait_recv()
        kv_copy(b).wait_send()
        return carry

    lax.fori_loop(0, NZ, kv_wait, 0)

    def a_copy(b, d):
        r = pl.ds(pl.multiple_of(b * rows, rows), rows)
        return remote(ab.at[m, r, :], ab.at[m, r, :], a_send.at[b, d], a_recv.at[b, m],
                      {"mp": (m + d) % 4, "seq": s})

    span = WINDOW_LENGTH + 256
    qi = lax.broadcasted_iota(jnp.int32, (rows, span), 0)
    ei = lax.broadcasted_iota(jnp.int32, (rows, span), 1)
    visible = (ei > qi) & (ei <= qi + WINDOW_LENGTH)

    def attend(b):
        r = pl.ds(pl.multiple_of(b * rows, rows), rows)
        rk = pl.ds(pl.multiple_of((2 * b + y) * 256, 256), span)
        keys = kv[rk, 0:128]
        vals = kv[rk, 128:256]
        for h in range(2):
            sc = lax.dot_general(qb[h, r, :], keys, (((1,), (1,)), ((), ())), preferred_element_type=f32)
            sc = jnp.where(visible, sc, -jnp.inf)
            top = jnp.max(sc, axis=-1, keepdims=True)
            p = jnp.exp(sc - top)
            tot = jnp.sum(p, axis=-1, keepdims=True)
            o = jnp.dot(p.astype(bf16), vals, preferred_element_type=f32)
            ab[m, r, h * 128:(h + 1) * 128] = (o / tot).astype(bf16)
        for d in range(1, 4):
            a_copy(b, d).start()

    def a_wait(b):
        r = pl.ds(pl.multiple_of(b * rows, rows), rows)
        for d in range(1, 4):
            mm = (m + d) % 4
            remote(ab.at[mm, r, :], ab.at[mm, r, :], a_send.at[b, d], a_recv.at[b, mm], ypeer).wait_recv()
            a_copy(b, d).wait_send()

    def partial(b, first, count):
        r = pl.ds(pl.multiple_of(b * rows + first, count), count)
        acc = jnp.dot(ab[0, r, :], ob[0], preferred_element_type=f32)
        for mm in range(1, NM):
            acc += jnp.dot(ab[mm, r, :], ob[mm], preferred_element_type=f32)
        return acc

    half = rows // 2

    def r_copy(side, b, hf, zd):
        r = pl.ds(hf * half, half)
        return remote(sb.at[b, r, :], rb.at[side, b, r, :], r_send.at[b, hf], r_recv.at[side, b, hf], at_z(zd))

    def hop(b):
        right = b > z
        side = jnp.where(right, 0, 1)
        target = jnp.where(right, (z + 1) % 4, (z + 3) % 4)
        inner = (right & (z > 0)) | (jnp.logical_not(right) & (z < 3))
        for hf in range(2):
            r = pl.ds(hf * half, half)
            pacc[r, :] = partial(b, hf * half, half)

            @pl.when(inner)
            def _():
                r_copy(side, b, hf, target).wait_recv()
                sb[b, r, :] = (pacc[r, :] + rb[side, b, r, :].astype(f32)).astype(bf16)

            @pl.when(jnp.logical_not(inner))
            def _():
                sb[b, r, :] = pacc[r, :].astype(bf16)

            r_copy(side, b, hf, target).start()

    def pick(a0, a1, a2, a3):
        return jnp.where(z == 0, a0, jnp.where(z == 1, a1, jnp.where(z == 2, a2, a3)))

    order = [pick(3, 3, 0, 0), pick(2, 0, 3, 1), pick(1, 2, 1, 2), z]
    edge = (z == 0) | (z == 3)

    def first_hop():
        a_wait(order[0])
        hop(order[0])

    attend(order[0])
    for h in range(2):
        o_in = ob.at[2 * (1 - y) + h]
        remote(o_in, o_in, oy_send.at[h], oy_recv.at[h], ypeer).wait_recv()
        own_o[h][1].wait()
    pl.when(edge)(first_hop)
    attend(order[1])
    pl.when(jnp.logical_not(edge))(first_hop)
    attend(order[2])
    a_wait(order[1])
    hop(order[1])
    attend(order[3])
    a_wait(order[2])
    hop(order[2])
    a_wait(order[3])

    pacc[...] = partial(z, 0, rows)
    for hf in range(2):
        r = pl.ds(hf * half, half)

        @pl.when(z > 0)
        def _():
            r_copy(0, z, hf, z).wait_recv()
            pacc[r, :] += rb[0, z, r, :].astype(f32)

        @pl.when(z < 3)
        def _():
            r_copy(1, z, hf, z).wait_recv()
            pacc[r, :] += rb[1, z, r, :].astype(f32)

    mixed = pacc[...]
    ss[m] = jnp.broadcast_to(jnp.sum(mixed * mixed, axis=-1, keepdims=True), (rows, 128))

    def s_copy(d):
        return remote(ss.at[m], ss.at[m], s_send.at[d], s_recv.at[m], {"mp": (m + d) % 4, "seq": s})

    for d in range(1, 4):
        s_copy(d).start()
    for d in range(1, 4):
        mm = (m + d) % 4
        remote(ss.at[mm], ss.at[mm], s_send.at[d], s_recv.at[mm], ypeer).wait_recv()
    squares = (ss[0] + ss[1] + ss[2] + ss[3])[:, 0:1]
    scaling = lax.rsqrt(squares / MODEL_WIDTH + epsilon)
    out[...] = (xb[z, m].astype(f32) + mixed * scaling * gain_post[...]).astype(bf16)

    for d in range(1, 4):
        s_copy(d).wait_send()
    for d in range(4):
        for hf in range(2):
            when(z != d, r_copy(0, d, hf, (z + 1) % 4).wait_send)
    for cond, cp in pending:
        when(cond, cp.wait_send)


def fused(
    hidden_in, gain_in, w_query, key_weight, value_weight, gain_query, gain_key, start_pos,
    cached_key_rows, cached_value_rows, w_out, gain_post,
):
    rows, cols = hidden_in.shape
    depth = w_query.shape[0]
    y = lax.axis_index("seq") % 2
    block = jnp.arange(4, dtype=jnp.int32)[:, None] * 2 + y
    positions = (start_pos[0] + block * rows + jnp.arange(rows, dtype=jnp.int32)[None, :]).reshape(-1)
    inverse_freq = rope_base ** (-(jnp.arange(64, dtype=f32) * 2.0) / 128)
    angles = positions.astype(f32)[:, None] * inverse_freq[None, :]
    cosine, sine = jnp.cos(angles), jnp.sin(angles)
    cos_t = jnp.concatenate([cosine, cosine], axis=1)
    sin_t = jnp.concatenate([-sine, sine], axis=1)
    hbm = pl.BlockSpec(memory_space=pl.ANY)
    vmem = pl.BlockSpec(memory_space=pltpu.VMEM)
    dma = pltpu.SemaphoreType.DMA
    return pl.pallas_call(
        layer_kernel,
        name="layer",
        out_shape=jax.ShapeDtypeStruct((rows, cols), bf16),
        in_specs=[hbm, vmem, hbm, hbm, hbm, vmem, vmem, vmem, vmem, hbm, hbm, hbm, vmem],
        out_specs=vmem,
        scratch_shapes=[
            pltpu.VMEM((4, 4, rows, cols), bf16),
            pltpu.VMEM((4, 4, rows, cols), bf16),
            pltpu.VMEM((4, depth, 512), bf16),
            pltpu.VMEM((4, 2 * depth, 512), bf16),
            pltpu.VMEM((4, 256, cols), bf16),
            pltpu.VMEM((3072, 256), bf16),
            pltpu.VMEM((2, 1024, 128), bf16),
            pltpu.VMEM((4, 1024, 256), bf16),
            pltpu.VMEM((2, 4, rows, cols), bf16),
            pltpu.VMEM((4, rows, cols), bf16),
            pltpu.VMEM((4, rows, 128), f32),
            pltpu.VMEM((rows, cols), f32),
            dma((9,)), dma((2, 4)), dma((4,)), dma((4,)), dma((4,)), dma((2, 4)), dma((2, 4)),
            dma((4, 3)), dma((4, 3)), dma((4,)), dma((4,)), dma((4,)), dma((4,)), dma((4, 2)), dma((2,)), dma((2,)), dma((2,)),
            dma((4,)), dma((4,)), dma((4, 4)), dma((4, 4)), dma((4, 2)), dma((2, 4, 2)), dma((4,)), dma((4,)),
        ],
        compiler_params=pltpu.CompilerParams(
            collective_id=0, has_side_effects=True, vmem_limit_bytes=60 * 1024 * 1024,
        ),
    )(
        hidden_in, gain_in.reshape(4, 1, cols), w_query, key_weight, value_weight,
        gain_query.reshape(1, 128), gain_key.reshape(1, 128), cos_t, sin_t,
        cached_key_rows, cached_value_rows, w_out, gain_post.reshape(1, cols),
    )


def shifted(x, axis, by):
    peers = lax.axis_size(axis)
    pairs = [(i, i + by) for i in range(peers) if 0 <= i + by < peers]
    return lax.ppermute(x, axis, pairs)


def norm_rows(values, gain):
    return values * lax.rsqrt(jnp.mean(values * values, axis=-1, keepdims=True) + epsilon) * gain


def rotate(tensor, positions):
    half_dim = tensor.shape[-1] // 2
    inverse_freq = rope_base ** (
        -(jnp.arange(half_dim, dtype=jnp.float32) * 2.0) / tensor.shape[-1]
    )
    angles = positions.astype(jnp.float32)[:, None, None] * inverse_freq[None, None, :]
    cosine = jnp.cos(angles)
    sine = jnp.sin(angles)
    first = tensor[..., :half_dim]
    second = tensor[..., half_dim:]
    return jnp.concatenate(
        [first * cosine - second * sine, second * cosine + first * sine], axis=-1
    )


def on_device(
    hidden_in,
    gain_in,
    w_query,
    key_weight,
    value_weight,
    gain_query,
    gain_key,
    start_pos,
    cached_key_rows,
    cached_value_rows,
    w_out,
    gain_post,
):
    n_rows = hidden_in.shape[0]
    head_dim = gain_query.shape[0]
    kv_cols = key_weight.shape[1]
    kv_heads = kv_cols // head_dim
    q_heads = w_query.shape[1] // head_dim
    query_group_count = q_heads // kv_heads
    full_rows = lax.all_gather(hidden_in, "mp", axis=1, tiled=True)
    normed_hidden = norm_rows(full_rows.astype(jnp.float32), gain_in).astype(jnp.bfloat16)

    def add_rows(block_rows):
        return jnp.dot(normed_hidden, block_rows, preferred_element_type=jnp.float32)

    keys_raw = add_rows(lax.all_gather(key_weight, "seq", axis=0, tiled=True))
    values_raw = add_rows(lax.all_gather(value_weight, "seq", axis=0, tiled=True))
    query_matrix = add_rows(lax.all_gather(w_query, "seq", axis=0, tiled=True))
    seq_index = lax.axis_index("seq")
    positions = start_pos[0] + seq_index * n_rows + jnp.arange(n_rows, dtype=jnp.int32)
    query_matrix = (
        rotate(norm_rows(query_matrix.reshape(n_rows, q_heads, head_dim), gain_query), positions)
        * query_scale
    ).astype(jnp.bfloat16)
    fresh_key = rotate(
        norm_rows(keys_raw.reshape(n_rows, kv_heads, head_dim), gain_key), positions
    ).astype(jnp.bfloat16)
    fresh = jnp.stack([fresh_key.reshape(n_rows, kv_cols), values_raw.astype(jnp.bfloat16)])
    reach_shards = (WINDOW_LENGTH + n_rows - 1) // n_rows
    reach_rows = reach_shards * n_rows
    pieces = []
    moving = fresh
    for hop_index in range(reach_shards):
        moving = shifted(moving, "seq", 1)
        pieces.insert(0, moving)
    prior = jnp.concatenate(pieces, axis=1)
    front_pad = reach_rows - WINDOW_LENGTH
    cached = jnp.stack([cached_key_rows, cached_value_rows])
    padded = jnp.concatenate(
        [
            jnp.zeros((2, front_pad, kv_cols), cached.dtype),
            cached,
            jnp.zeros((2, reach_rows, kv_cols), cached.dtype),
        ],
        axis=1,
    )
    cache_start = jnp.minimum(seq_index * n_rows, front_pad + WINDOW_LENGTH)
    from_cache = lax.dynamic_slice_in_dim(padded, cache_start, reach_rows, 1)
    prior_rows = jnp.arange(reach_rows, dtype=jnp.int32)
    use_cache = prior_rows < reach_rows - seq_index * n_rows
    prior = jnp.where(use_cache[None, :, None], from_cache, prior)
    window_kv = jnp.concatenate([prior, fresh], axis=1)
    span_rows = reach_rows + n_rows
    key_heads = window_kv[0].reshape(span_rows, kv_heads, head_dim)
    value_heads = window_kv[1].reshape(span_rows, kv_heads, head_dim)
    query_heads = query_matrix.reshape(n_rows, kv_heads, query_group_count, head_dim)
    scores = jnp.einsum(
        "tkgd,skd->kgts", query_heads, key_heads, preferred_element_type=jnp.float32
    )
    query_index = jnp.arange(n_rows, dtype=jnp.int32)[:, None]
    key_index = jnp.arange(span_rows, dtype=jnp.int32)[None, :]
    visible = (key_index > query_index + reach_rows - WINDOW_LENGTH) & (
        key_index <= query_index + reach_rows
    )
    scores = jnp.where(visible, scores, -jnp.inf)
    row_max = jnp.max(scores, axis=-1, keepdims=True)
    probs = jnp.exp(scores - row_max)
    totals = jnp.sum(probs, axis=-1)
    probs_b = probs.astype(jnp.bfloat16)
    summed = jnp.einsum("kgts,skd->tkgd", probs_b, value_heads, preferred_element_type=jnp.float32)
    summed = summed / jnp.transpose(totals, (2, 0, 1))[..., None]
    attn = summed.reshape(n_rows, q_heads * head_dim).astype(jnp.bfloat16)
    all_heads = lax.all_gather(attn, "mp", axis=1, tiled=True)
    projected = jnp.dot(
        all_heads,
        lax.all_gather(w_out, "seq", axis=0, tiled=True),
        preferred_element_type=jnp.float32,
    )
    squares = lax.psum(jnp.sum(projected * projected, axis=-1), "mp")
    scaling = lax.rsqrt(squares / MODEL_WIDTH + epsilon)
    return (hidden_in.astype(jnp.float32) + projected * scaling[:, None] * gain_post).astype(
        jnp.bfloat16
    )


def solution(mesh):
    in_specs = (
        P("seq", "mp"),
        P(),
        P("seq", "mp"),
        P("seq", "mp"),
        P("seq", "mp"),
        P(),
        P(),
        P(),
        P(None, "mp"),
        P(None, "mp"),
        P("seq", "mp"),
        P("mp"),
    )
    out_specs = P("seq", "mp")
    fits = mesh.shape["mp"] == 4 and mesh.shape["seq"] == 8
    return jax.shard_map(
        fused if fits else on_device, mesh=mesh, in_specs=in_specs, out_specs=out_specs, check_vma=False
    )
```
